128 devices in a mesh: slab: 16 (over z, y_hi, core), deal: 8 (over x, y_lo).
Axes of the slice: x: 4, y: 4 (y_hi: 2, y_lo: 2; y = y_hi * 2 + y_lo), z: 4, core: 2. Of those that a mesh axis runs over, the one named last changes fastest.
Arguments:
- offsets: float32 [131072, 3, 128], P(('slab', 'deal')), may hold values from -0.5 to 0.5
- velocity: float32 [131072, 3, 128], P(('slab', 'deal')), may hold values from -6 to 6
- affine: float32 [131072, 9, 128], P(('slab', 'deal')), may hold values from -6 to 6
- particle_mass: float32 [131072, 128], P(('slab', 'deal')), may hold values from 0.5 to 2
- cell_in_tile: int32 [131072, 128], P(('slab', 'deal')), may hold values from 0 to 255
- block_tile: int32 [131072], P(('slab', 'deal')), may hold values from 0 to 2047, as said below
- live_blocks: int32 [16, 8], P('slab', 'deal'), may hold values from 512 to 1024, as said below
- send_lists: int32 [16, 8, 2, 16], P('slab', 'deal'), may hold values from 0 to 1023, as said below
- send_counts: int32 [16, 8, 2], P('slab', 'deal'), may hold values from 0 to 16, as said below
Outputs:
- updated_particles: float32 [131072, 15, 128], P(('slab', 'deal'))
- arrivals: float32 [16, 8, 2, 16, 16, 128], P('slab', 'deal')
- grid_velocity: float32 [3, 1024, 8192], P(None, 'slab', 'deal')
The draws below stay inside these ranges and needn't reach their ends.
Inputs may be any that keep to these rules, and one draw needn't show every extreme that they name: `block_tile`: blocks are sorted by cell: on device (s, d) the tiles never fall along its blocks and lie in [max(d * R - M, 0), min((d + 1) * R + M, 2048)) with R = 256 and M = max(R // 16, 1); some device with d > 0 reaches d * R - M. `live_blocks`: some device has all 1024 blocks live. `send_lists`: the 32 entries of one device's two lists are distinct blocks of that device. `send_counts`: counts toward a slab beyond the ends are zero; some device sends 16 blocks downslope.
All inputs are finite; a program needn't handle non-finite values.
Results may differ from the reference program's by a relative error of at most 0.000073.
Values sent between devices are 32-bit elements; how exact they have to be, the bound alone decides.
No kernel may reach another device: no remote copies, remote signals or barrier semaphores. Data moves between devices by JAX's collectives and lax.ppermute only.
A program may use at most 128 MiB of HBM per device.

```python
import math
import jax
import jax.numpy as jnp

NB = 1024
PX = 64
PLANE = 8192
TILE = 256
MIG = 16
SLABS = 16
DEALS = 8
BLOCKS = 131072
N_SLAB = 16
N_DEAL = 8


def draw_block_tile(key, part):
    tile_count = PX * PLANE // TILE
    share = tile_count // DEALS
    margin = max(share // 16, 1)
    key_raw, key_slab, key_deal = jax.random.split(jax.random.fold_in(key, 11), 3)
    deal_ids = jnp.arange(DEALS, dtype=jnp.int32)[None, :, None]
    lowest = jnp.maximum(deal_ids * share - margin, 0)
    highest = jnp.minimum((deal_ids + 1) * share + margin, tile_count)
    raw = jax.random.randint(key_raw, (SLABS, DEALS, NB), 0, 1 << 20)
    tiles = lowest + raw % (highest - lowest)
    tiles = jnp.sort(tiles, axis=-1)
    pick_slab = jax.random.randint(key_slab, (), 0, SLABS)
    pick_deal = jax.random.randint(key_deal, (), 1, DEALS)
    forced = (jnp.arange(SLABS)[:, None, None] == pick_slab) & (deal_ids == pick_deal) & (jnp.arange(NB)[None, None, :] == 0)
    tiles = jnp.where(forced, lowest, tiles)
    return tiles.reshape(BLOCKS).astype(jnp.int32)


def draw_live_blocks(key, part):
    key_counts, key_slab, key_deal = jax.random.split(key, 3)
    counts = jax.random.randint(key_counts, (SLABS, DEALS), NB // 2, NB + 1)
    pick_slab = jax.random.randint(key_slab, (), 0, SLABS)
    pick_deal = jax.random.randint(key_deal, (), 0, DEALS)
    chosen_cell = (jnp.arange(SLABS)[:, None] == pick_slab) & (jnp.arange(DEALS)[None, :] == pick_deal)
    return jnp.where(chosen_cell, NB, counts).astype(jnp.int32)


def draw_send_lists(key, part):
    scores = jax.random.randint(key, (SLABS, DEALS, NB), 0, 1 << 16)
    distinct = scores * NB + jnp.arange(NB, dtype=jnp.int32)
    ordering = jnp.argsort(distinct, axis=-1)
    return ordering[:, :, :2 * MIG].reshape(SLABS, DEALS, 2, MIG).astype(jnp.int32)


def draw_send_counts(key, part):
    key_counts, key_slab, key_deal = jax.random.split(key, 3)
    counts = jax.random.randint(key_counts, (SLABS, DEALS, 2), 0, MIG + 1)
    slab_ids = jnp.arange(SLABS)[:, None, None]
    deal_ids = jnp.arange(DEALS)[None, :, None]
    directions = jnp.arange(2)[None, None, :]
    counts = jnp.where((directions == 0) & (slab_ids == SLABS - 1), 0, counts)
    counts = jnp.where((directions == 1) & (slab_ids == 0), 0, counts)
    pick_slab = jax.random.randint(key_slab, (), 0, SLABS - 1)
    pick_deal = jax.random.randint(key_deal, (), 0, DEALS)
    forced = (slab_ids == pick_slab) & (deal_ids == pick_deal) & (directions == 0)
    return jnp.where(forced, MIG, counts).astype(jnp.int32)


def with_ends(drawn, key, least, top_value):
    longest = drawn.shape.index(max(drawn.shape))
    spots = []
    for shift in (0, 1):
        where = [jax.random.randint(jax.random.fold_in(key, axis), (), 0, length) for axis, length in enumerate(drawn.shape)]
        where[longest] = (where[longest] + shift) % drawn.shape[longest]
        spots.append(tuple(where))
    return drawn.at[spots[0]].set(least).at[spots[1]].set(top_value)


def level_of(key, shape, shards, low, largest):
    def one(position, blocks):
        steps = jax.random.uniform(jax.random.fold_in(jax.random.fold_in(key, 6), position), (blocks,), jnp.float32, low / len(shards), largest / len(shards))
        return jnp.repeat(jnp.exp(steps), shape[position] // blocks).reshape((-1,) + (1,) * (len(shape) - position - 1))

    loudness = one(*shards[0])
    for cut in shards[1:]:
        loudness = loudness * one(*cut)
    return loudness


def noise(key, shape, spread, most, cuts=(), kind=jnp.bfloat16):
    gain = level_of(key, shape, cuts, -0.22, 0.18) if cuts else 1.0
    entries = jax.random.normal(key, shape, jnp.float32) * spread * gain
    return jnp.minimum(jnp.maximum(entries, -most), most).astype(kind)


def setup_inputs(seed: int = 0) -> dict:
    splits = jax.random.split(jax.random.key(seed), 10)
    return {
        "offsets": jnp.clip(jax.random.uniform(splits[0], (BLOCKS, 3, 128), jnp.float32, -0.5, 0.5) * level_of(splits[0], (BLOCKS, 3, 128), ((0, 128),), -0.4, 0.0), -0.5, 0.5),
        "velocity": noise(splits[1], (BLOCKS, 3, 128), 1.0, 6.0, ((0, 128),), jnp.float32),
        "affine": noise(splits[2], (BLOCKS, 9, 128), 1.0, 6.0, ((0, 128),), jnp.float32),
        "particle_mass": jnp.clip(jnp.exp(math.log(2.0) - 1.3862944 * jax.random.uniform(splits[3], (BLOCKS, 128), jnp.float32) ** level_of(splits[3], (BLOCKS, 128), ((0, 128),), -0.2, 0.2)), 0.5, 2.0),
        "cell_in_tile": with_ends(jax.random.randint(splits[4], (BLOCKS, 128), 0, TILE), jax.random.fold_in(splits[4], 1), 0, TILE - 1).astype(jnp.int32),
        "block_tile": draw_block_tile(jax.random.fold_in(splits[9], 71), 0),
        "live_blocks": draw_live_blocks(jax.random.fold_in(splits[9], 71), 0),
        "send_lists": draw_send_lists(jax.random.fold_in(splits[9], 71), 0),
        "send_counts": draw_send_counts(jax.random.fold_in(splits[9], 71), 0),
    }


time_step = 0.1
viscosity = 0.2
gravity_pull = (3.0, 0.0, -5.0)


def momentum(offsets, velocity, affine):
    columns = []
    for column in range(3):
        total = velocity[:, column]
        for inner in range(3):
            total = total - affine[:, 3 * column + inner] * offsets[:, inner]
        columns.append(total)
    return jnp.stack(columns, axis=1)


def grid_update(summed):
    floor_mass = jnp.maximum(summed[0], 1.0)
    speeds = []
    for column in range(3):
        speeds.append(summed[1 + column] / floor_mass + time_step * gravity_pull[column])
    return jnp.stack(speeds, axis=0)


def smooth_planes(speed, padded):
    return speed + viscosity * (padded[:, 2:] + padded[:, :-2] - 2.0 * speed)


def new_state(offsets, moved):
    shifted = offsets + time_step * moved
    affine_rows = []
    for column in range(3):
        for inner in range(3):
            affine_rows.append(-4.0 * moved[:, column] * offsets[:, inner])
    return jnp.concatenate([shifted, moved, jnp.stack(affine_rows, axis=1)], axis=1)


def reference(offsets, velocity, affine, particle_mass, cell_in_tile, block_tile, live_blocks, send_lists, send_counts):
    cells_slab = PX * PLANE
    block_ids = jnp.arange(BLOCKS, dtype=jnp.int32)
    slab_of = block_ids // (NB * N_DEAL)
    live_flat = live_blocks.reshape(-1)
    active = ((block_ids % NB) < live_flat[block_ids // NB]).astype(jnp.float32)
    flat_cell = slab_of[:, None] * cells_slab + block_tile[:, None] * TILE + cell_in_tile
    weight = particle_mass * active[:, None]
    moment = momentum(offsets, velocity, affine)
    deposit = jnp.concatenate([weight[:, None, :], weight[:, None, :] * moment], axis=1)
    summed = jax.ops.segment_sum(jnp.transpose(deposit, (0, 2, 1)).reshape(-1, 4), flat_cell.reshape(-1), num_segments=N_SLAB * cells_slab)
    summed = summed.T.reshape(4, N_SLAB * PX, PLANE)
    speed = grid_update(summed)
    padded = jnp.pad(speed, ((0, 0), (1, 1), (0, 0)))
    settled = smooth_planes(speed, padded)
    picked = settled.reshape(3, -1)[:, flat_cell]
    moved = jnp.transpose(picked, (1, 0, 2))
    state = new_state(offsets, moved)
    records = jnp.concatenate([state, particle_mass[:, None, :]], axis=1)
    device_ids = jnp.arange(N_SLAB * N_DEAL, dtype=jnp.int32).reshape(N_SLAB, N_DEAL)
    gather_ids = device_ids[:, :, None, None] * NB + send_lists
    leaving = records[gather_ids]
    slots = jnp.arange(MIG, dtype=jnp.int32)
    keeping = (slots[None, None, None, :] < send_counts[..., None]).astype(jnp.float32)
    leaving = leaving * keeping[..., None, None]
    empty = jnp.zeros_like(leaving[:1, :, 0])
    from_left = jnp.concatenate([empty, leaving[:-1, :, 0]], axis=0)
    from_right = jnp.concatenate([leaving[1:, :, 1], empty], axis=0)
    arrivals = jnp.stack([from_left, from_right], axis=2)
    return state, arrivals, settled
```

```python
import functools

import jax
import jax.numpy as jnp
from jax import lax
from jax.experimental import pallas as pl
from jax.experimental.pallas import tpu as pltpu
from jax.sharding import PartitionSpec as P

time_step = 0.1
viscosity = 0.2
gravity_pull = (3.0, 0.0, -5.0)

LANES = 128
ROWS = 8
PLANE_TILES = 32
SHARE = 256
MARGIN = 16
REACH = MARGIN + PLANE_TILES
EXTENT = SHARE + 2 * REACH
BAND = REACH + MARGIN
MOVED = SHARE + 2 * MARGIN
NB = 1024
STEP = 128
GROUPS = 8
UNIT = 64
MIG = 16


def in_hbm(*arrays):
    return [pltpu.with_memory_space_constraint(x, pltpu.HBM) for x in arrays]


def in_vmem(x):
    return pltpu.with_memory_space_constraint(x, pltpu.VMEM)


def first_block_at(tile_ref, tile):
    def halve(i, span):
        low, high = span
        middle = (low + high) // 2
        below = tile_ref[jnp.minimum(middle, NB - 1)] < tile
        more = low < high
        return (
            jnp.where(more & below, middle + 1, low),
            jnp.where(more & jnp.logical_not(below), middle, high),
        )

    return lax.fori_loop(0, 11, halve, (jnp.int32(0), jnp.int32(NB)))[0]


def deposit_kernel(
    outer, shift_ref, tile_ref, live_ref, off_hbm, vel_hbm, aff_hbm, mass_hbm, cell_hbm,
    *rest,
):
    if outer:
        sums_ref, onward_ref, backward_ref = rest[:3]
        rest = rest[3:]
    else:
        sums_ref = rest[0]
        rest = rest[1:]
    off_ref, vel_ref, aff_ref, mass_ref, cell_ref, second_ref, parts_ref, slots_ref, late_ref, sems = rest
    live = live_ref[0, 0]
    shift = shift_ref[0]
    units = NB // UNIT
    left_end = lax.div(first_block_at(tile_ref, shift + REACH - MARGIN + BAND) + (UNIT - 1), UNIT)
    right_start = jnp.maximum(lax.div(first_block_at(tile_ref, shift + SHARE), UNIT), left_end)

    per = STEP // UNIT
    chunks = NB // STEP

    def copies(chunk):
        rows = pl.ds(pl.multiple_of(chunk * STEP, STEP), STEP)
        return [
            pltpu.make_async_copy(off_hbm.at[:, rows, :], off_ref.at[:, rows, :], sems.at[chunk, 0]),
            pltpu.make_async_copy(vel_hbm.at[:, rows, :], vel_ref.at[:, rows, :], sems.at[chunk, 1]),
            pltpu.make_async_copy(aff_hbm.at[:, rows, :], aff_ref.at[:, rows, :], sems.at[chunk, 2]),
            pltpu.make_async_copy(mass_hbm.at[rows, :], mass_ref.at[rows, :], sems.at[chunk, 3]),
            pltpu.make_async_copy(cell_hbm.at[rows, :], cell_ref.at[rows, :], sems.at[chunk, 4]),
        ]

    def begin(chunk, carry):
        first, last = chunk * per, (chunk + 1) * per
        if outer:
            needed = (first < left_end) | (last > right_start)
        else:
            needed = jnp.maximum(first, left_end) < jnp.minimum(last, right_start)

        @pl.when(needed)
        def _():
            for copy in copies(chunk):
                copy.start()

        return carry

    lax.fori_loop(0, chunks, begin, 0)

    def clear(i, carry):
        nothing = jnp.zeros((8, ROWS, LANES), jnp.float32)
        sums_ref[pl.ds(i * 8, 8)] = nothing
        second_ref[pl.ds(i * 8, 8)] = nothing
        return carry

    lax.fori_loop(0, EXTENT // 8, clear, 0)

    slot_ids = lax.broadcasted_iota(jnp.int32, (LANES, LANES), 0).astype(jnp.bfloat16)
    block_ids = lax.broadcasted_iota(jnp.int32, (8, LANES), 0)
    one = jnp.ones((LANES, LANES), jnp.bfloat16)
    zero = jnp.zeros((LANES, LANES), jnp.bfloat16)
    blank = jnp.zeros((16, LANES), jnp.bfloat16)

    def settle(before):
        for b in range(0, UNIT, 2):
            tile_a = tile_ref[before * UNIT + b] - shift
            tile_b = tile_ref[before * UNIT + b + 1] - shift
            sums_ref[tile_a] = sums_ref[tile_a] + late_ref[b]
            second_ref[tile_b] = second_ref[tile_b] + late_ref[b + 1]

    def clear_late(i, carry):
        late_ref[pl.ds(i * 8, 8)] = jnp.zeros((8, ROWS, LANES), jnp.float32)
        return carry

    lax.fori_loop(0, UNIT // 8, clear_late, 0)

    def unit(v, before):
        if outer:
            i = jnp.where(v < left_end, v, v - left_end + right_start)
        else:
            i = v + left_end
        chunk = lax.div(i, per)
        fresh = chunk * per == i
        if outer:
            fresh = fresh | ((v == left_end) & (chunk * per >= left_end))
        else:
            fresh = fresh | (v == 0)

        @pl.when(fresh)
        def _():
            for copy in copies(chunk):
                copy.wait()

        settle(before)
        for u in range(UNIT // 8):
            base = pl.multiple_of(i * UNIT + u * 8, 8)
            rows = pl.ds(base, 8)
            off = [off_ref[c, rows, :] for c in range(3)]
            weight = jnp.where((block_ids + base) < live, mass_ref[rows, :], 0.0)
            parts = [weight]
            for c in range(3):
                total = vel_ref[c, rows, :]
                for k in range(3):
                    total = total - aff_ref[3 * c + k, rows, :] * off[k]
                parts.append(weight * total)
            cell = cell_ref[rows, :]
            upper = cell >= LANES
            slots_ref[u] = (cell & (LANES - 1)).astype(jnp.float32)
            for c in range(4):
                parts_ref[u, pl.ds(c * 8, 8), :] = jnp.where(upper, 0.0, parts[c])
                parts_ref[u, pl.ds((4 + c) * 8, 8), :] = jnp.where(upper, parts[c], 0.0)

            def prepared(b):
                slot = slots_ref[u, pl.ds(b, 8, stride=0), :]
                slot = jnp.concatenate([slot, slot], axis=0).astype(jnp.bfloat16)
                slot = jnp.concatenate([slot] * 8, axis=0)
                chosen = jnp.where(slot == slot_ids, one, zero)
                part = parts_ref[u, pl.ds(b, 8, stride=8), :]
                high = part.astype(jnp.bfloat16).astype(jnp.float32)
                split = jnp.concatenate([high, part - high], axis=0).astype(jnp.bfloat16)
                return split, chosen

            for b in range(0, 8, 2):
                split_a, chosen_a = prepared(b)
                split_b, chosen_b = prepared(b + 1)
                split = jnp.concatenate(
                    [
                        jnp.concatenate([split_a, blank], axis=1),
                        jnp.concatenate([blank, split_b], axis=1),
                    ],
                    axis=0,
                )
                chosen = jnp.concatenate([chosen_a, chosen_b], axis=1)
                both = lax.dot_general(
                    split, chosen, (((1,), (1,)), ((), ())),
                    preferred_element_type=jnp.float32,
                )
                late_ref[u * 8 + b] = both[:8] + both[8:16]
                late_ref[u * 8 + b + 1] = both[16:24] + both[24:]
        return i

    count = left_end + (units - right_start) if outer else right_start - left_end
    settle(lax.fori_loop(0, count, unit, jnp.int32(0)))

    def join(i, carry):
        rows = pl.ds(i * 8, 8)
        sums_ref[rows] = sums_ref[rows] + second_ref[rows]
        return carry

    lax.fori_loop(0, EXTENT // 8, join, 0)

    if outer:

        def send(i, carry):
            onward_ref[pl.ds(i * 8, 8)] = sums_ref[pl.ds(SHARE + i * 8, 8)]
            backward_ref[pl.ds(i * 8, 8)] = sums_ref[pl.ds(REACH - MARGIN + i * 8, 8)]
            return carry

        lax.fori_loop(0, BAND // 8, send, 0)


def deposit(outer, shift, block_tile, live_blocks, offsets, velocity, affine, particle_mass, cells):
    smem = pl.BlockSpec(memory_space=pltpu.SMEM)
    hbm = pl.BlockSpec(memory_space=pltpu.HBM)
    vmem = pl.BlockSpec(memory_space=pltpu.VMEM)
    shapes = [EXTENT, BAND, BAND] if outer else [EXTENT]
    return pl.pallas_call(
        functools.partial(deposit_kernel, outer),
        in_specs=[smem] * 3 + [hbm] * 5,
        out_specs=[vmem] * len(shapes),
        out_shape=[jax.ShapeDtypeStruct((n, ROWS, LANES), jnp.float32) for n in shapes],
        scratch_shapes=[
            pltpu.VMEM((3, NB, LANES), jnp.float32),
            pltpu.VMEM((3, NB, LANES), jnp.float32),
            pltpu.VMEM((9, NB, LANES), jnp.float32),
            pltpu.VMEM((NB, LANES), jnp.float32),
            pltpu.VMEM((NB, LANES), jnp.int32),
            pltpu.VMEM((EXTENT, ROWS, LANES), jnp.float32),
            pltpu.VMEM((UNIT // 8, 64, LANES), jnp.float32),
            pltpu.VMEM((UNIT // 8, 8, LANES), jnp.float32),
            pltpu.VMEM((UNIT, ROWS, LANES), jnp.float32),
            pltpu.SemaphoreType.DMA((NB // STEP, 5)),
        ],
        compiler_params=pltpu.CompilerParams(vmem_limit_bytes=40 << 20),
        cost_estimate=pl.CostEstimate(
            flops=NB * 16 * LANES * LANES, bytes_accessed=10 << 20, transcendentals=0
        ),
        name="deposit_outer" if outer else "deposit_inner",
    )(shift, block_tile, live_blocks, *in_hbm(offsets, velocity, affine, particle_mass, cells))


def gather_blocks(tiles_of, row_of, moved_ref, found_ref, cell_ref, base, slot):
    for b in range(8):
        place = row_of(b)
        index = cell_ref[pl.ds(base + b, 8, stride=0), :] & (LANES - 1)
        found_ref[slot, pl.ds(b * 8, 8), :] = jnp.take_along_axis(
            moved_ref[place], index, axis=1
        )
    upper = cell_ref[pl.ds(base, 8), :] >= LANES
    return [
        jnp.where(
            upper,
            found_ref[slot, pl.ds(5 + c, 8, stride=8), :],
            found_ref[slot, pl.ds(1 + c, 8, stride=8), :],
        )
        for c in range(3)
    ]


def state_of(off, vel):
    state = [off[c] + time_step * vel[c] for c in range(3)] + list(vel)
    for c in range(3):
        scaled = -4.0 * vel[c]
        for k in range(3):
            state.append(scaled * off[k])
    return state


def grid_kernel(
    shift_ref, ends_ref, tile_ref, list_ref, count_ref,
    sums_ref, inner_ref, left_ref, right_ref, off_ref, mass_ref, cell_ref,
    moved_ref, share_ref, onward_ref, backward_ref,
    total_ref, speed_ref, flat_ref, pick_ref, pick_cell_ref, found_ref,
):
    row_ids = lax.broadcasted_iota(jnp.int32, (ROWS, LANES), 0)
    lower_half = row_ids < 4
    channel = row_ids & 3
    pull = jnp.where(
        channel == 1,
        time_step * gravity_pull[0],
        jnp.where(channel == 3, time_step * gravity_pull[2], time_step * gravity_pull[1]),
    ).astype(jnp.float32)

    def rows_of(j):
        return pl.ds(pl.multiple_of(j * ROWS, ROWS), ROWS)

    def load_left(j):
        total_ref[rows_of(j), :] = sums_ref[j] + inner_ref[j] + left_ref[j]

    def load_middle(j):
        total_ref[rows_of(j), :] = sums_ref[j] + inner_ref[j]

    def load_right(j):
        total_ref[rows_of(j), :] = sums_ref[j] + inner_ref[j] + right_ref[j - (EXTENT - BAND)]

    def over(first, count, body, unroll=8):
        def some(i, carry):
            for u in range(unroll):
                body(first + i * unroll + u)
            return carry

        lax.fori_loop(0, count // unroll, some, 0)

    over(0, BAND, load_left)
    over(BAND, EXTENT - 2 * BAND, load_middle)
    over(EXTENT - BAND, BAND, load_right)

    def speeds(j):
        total = total_ref[rows_of(j), :]
        mass = jnp.where(
            lower_half,
            total_ref[pl.ds(j * ROWS, ROWS, stride=0), :],
            total_ref[pl.ds(j * ROWS + 4, ROWS, stride=0), :],
        )
        speed_ref[j] = total / jnp.maximum(mass, 1.0) + pull

    over(0, EXTENT, speeds)

    @pl.when(ends_ref[0] == 1)
    def _():
        def none(j):
            speed_ref[j] = jnp.zeros((ROWS, LANES), jnp.float32)

        over(0, REACH, none)

    @pl.when(ends_ref[0] == 2)
    def _():
        def none(j):
            speed_ref[j] = jnp.zeros((ROWS, LANES), jnp.float32)

        over(EXTENT - REACH, REACH, none)

    def smooth(j):
        here = speed_ref[j + PLANE_TILES]
        settled = here + viscosity * (
            speed_ref[j + 2 * PLANE_TILES] + speed_ref[j] - 2.0 * here
        )
        moved_ref[j] = settled
        flat_ref[rows_of(j), :] = settled

    over(0, MOVED, smooth)

    planes = SHARE // PLANE_TILES
    for dest in range(8):
        for c in range(3):
            for q in range(8):
                tile = MARGIN + 4 * dest + q // 2
                start = tile * ROWS + (q % 2) * 4 + 1 + c
                share_ref[dest, c, :, pl.ds(q * LANES, LANES)] = flat_ref[
                    pl.ds(start, planes, stride=PLANE_TILES * ROWS), :
                ]

    shift = shift_ref[0]
    for side, leave_ref in enumerate((onward_ref, backward_ref)):
        for first in range(0, MIG, 8):
            blocks = [list_ref[0, 0, side, first + b] for b in range(8)]
            for b in range(8):
                row = pl.ds(blocks[b], 1)
                for c in range(3):
                    pick_ref[c, pl.ds(b, 1), :] = off_ref[c, row, :]
                pick_ref[3, pl.ds(b, 1), :] = mass_ref[row, :]
                pick_cell_ref[pl.ds(b, 1), :] = cell_ref[row, :]
            vel = gather_blocks(
                None, lambda b: tile_ref[blocks[b]] - shift, moved_ref, found_ref,
                pick_cell_ref, 0, 0,
            )
            off = [pick_ref[c] for c in range(3)]
            record = state_of(off, vel) + [pick_ref[3]]
            keep = (row_ids + first) < count_ref[0, 0, side]
            for c in range(16):
                rows = pl.ds(first * 16 + c, 8, stride=16)
                leave_ref[rows, :] = jnp.where(keep, record[c], 0.0)


def grid_step(shift, ends, block_tile, lists, counts, sums, inner, left, right, offsets, mass, cells):
    smem = pl.BlockSpec(memory_space=pltpu.SMEM)
    vmem = pl.BlockSpec(memory_space=pltpu.VMEM)
    planes = SHARE // PLANE_TILES
    return pl.pallas_call(
        grid_kernel,
        in_specs=[smem] * 5 + [vmem] * 7,
        out_specs=[vmem] * 4,
        out_shape=[
            jax.ShapeDtypeStruct((MOVED, ROWS, LANES), jnp.float32),
            jax.ShapeDtypeStruct((8, 3, planes, 8 * LANES), jnp.float32),
            jax.ShapeDtypeStruct((MIG * 16, LANES), jnp.float32),
            jax.ShapeDtypeStruct((MIG * 16, LANES), jnp.float32),
        ],
        scratch_shapes=[
            pltpu.VMEM((EXTENT * ROWS, LANES), jnp.float32),
            pltpu.VMEM((EXTENT, ROWS, LANES), jnp.float32),
            pltpu.VMEM((MOVED * ROWS, LANES), jnp.float32),
            pltpu.VMEM((4, 8, LANES), jnp.float32),
            pltpu.VMEM((8, LANES), jnp.int32),
            pltpu.VMEM((1, 64, LANES), jnp.float32),
        ],
        compiler_params=pltpu.CompilerParams(vmem_limit_bytes=24 << 20),
        cost_estimate=pl.CostEstimate(flops=1 << 22, bytes_accessed=8 << 20, transcendentals=0),
        name="grid_step",
    )(shift, ends, block_tile, lists, counts, sums, inner, left, right, offsets, mass, cells)


def update_kernel(shift_ref, tile_ref, moved_ref, off_ref, cell_ref, state_ref, found_ref):
    step = pl.program_id(0)
    shift = shift_ref[0]

    def group(i, carry):
        for u in range(GROUPS):
            base = pl.multiple_of((i * GROUPS + u) * 8, 8)
            rows = pl.ds(base, 8)
            vel = gather_blocks(
                None, lambda b: tile_ref[step * STEP + base + b] - shift, moved_ref,
                found_ref, cell_ref, base, u,
            )
            off = [off_ref[c, rows, :] for c in range(3)]
            state = state_of(off, vel)
            for c in range(15):
                state_ref[c, rows, :] = state[c]
        return carry

    lax.fori_loop(0, STEP // (8 * GROUPS), group, 0)


def update(shift, block_tile, moved, offsets, cells):
    smem = pl.BlockSpec(memory_space=pltpu.SMEM)
    return pl.pallas_call(
        update_kernel,
        grid=(NB // STEP,),
        in_specs=[
            smem,
            smem,
            pl.BlockSpec((MOVED, ROWS, LANES), lambda i: (0, 0, 0)),
            pl.BlockSpec((3, STEP, LANES), lambda i: (0, i, 0)),
            pl.BlockSpec((STEP, LANES), lambda i: (i, 0)),
        ],
        out_specs=pl.BlockSpec((15, STEP, LANES), lambda i: (0, i, 0)),
        out_shape=jax.ShapeDtypeStruct((15, NB, LANES), jnp.float32),
        scratch_shapes=[pltpu.VMEM((GROUPS, 64, LANES), jnp.float32)],
        compiler_params=pltpu.CompilerParams(vmem_limit_bytes=16 << 20),
        cost_estimate=pl.CostEstimate(flops=1 << 22, bytes_accessed=12 << 20, transcendentals=0),
        name="update",
    )(shift, block_tile, in_vmem(moved), *in_hbm(offsets, cells))


def body(
    offsets, velocity, affine, particle_mass, cell_in_tile, block_tile, live_blocks,
    send_lists, send_counts,
):
    deals, slabs = lax.axis_size("deal"), lax.axis_size("slab")
    deal, slab = lax.axis_index("deal"), lax.axis_index("slab")
    place = slab * deals + deal
    off = jnp.transpose(offsets, (1, 0, 2))
    vel = jnp.transpose(velocity, (1, 0, 2))
    aff = jnp.transpose(affine, (1, 0, 2))
    wide = (deal * SHARE - REACH).astype(jnp.int32).reshape(1)
    near = (deal * SHARE - MARGIN).astype(jnp.int32).reshape(1)
    ends = jnp.where(place == 0, 1, jnp.where(place == slabs * deals - 1, 2, 0))
    ends = ends.astype(jnp.int32).reshape(1)
    particles = (wide, block_tile, live_blocks, off, vel, aff, particle_mass, cell_in_tile)
    sums, to_next, to_last = deposit(True, *particles)
    count = slabs * deals
    onward = [(i, i + 1) for i in range(count - 1)]
    backward = [(j, i) for i, j in onward]
    axes = ("slab", "deal")
    left = lax.ppermute(to_next, axes, onward)
    right = lax.ppermute(to_last, axes, backward)
    inner, = deposit(False, *particles)
    moved, share, ahead, behind = grid_step(
        near, ends, block_tile, send_lists, send_counts, sums, inner, left, right, off,
        particle_mass, cell_in_tile,
    )
    ahead, behind = [x.reshape(MIG, 16, LANES) for x in (ahead, behind)]
    down = [(i, i + 1) for i in range(slabs - 1)]
    up = [(j, i) for i, j in down]
    from_left = lax.ppermute(ahead, "slab", down)
    from_right = lax.ppermute(behind, "slab", up)
    own = lax.all_to_all(share, "deal", 0, 0, tiled=True)
    state = update(near, block_tile, moved, off, cell_in_tile)
    arrivals = jnp.stack([from_left, from_right], axis=0)[None, None]
    own = jnp.transpose(own, (1, 0, 2, 3)).reshape(3, deals * (SHARE // PLANE_TILES), 8 * LANES)
    return jnp.transpose(state, (1, 0, 2)), arrivals, own


def solution(mesh):
    both = ("slab", "deal")
    placed = (
        P(both, None, None),
        P(both, None, None),
        P(both, None, None),
        P(both, None),
        P(both, None),
        P(both),
        P("slab", "deal"),
        P("slab", "deal", None, None),
        P("slab", "deal", None),
    )
    return jax.shard_map(
        body,
        mesh=mesh,
        in_specs=placed,
        out_specs=(
            P(both, None, None),
            P("slab", "deal", None, None, None, None),
            P(None, "slab", "deal"),
        ),
        check_vma=False,
    )
```
